512 devices in a mesh: dp: 8 (over y, core), station: 64 (over x, z).
Axes of the slice: x: 4, y: 4, z: 16, core: 2. Of those that a mesh axis runs over, the one named last changes fastest.
Arguments:
- query_states: bfloat16 [8, 64, 128, 768], P('dp', 'station'), may hold values from -6 to 6
- key_states: bfloat16 [8, 64, 128, 768], P('dp', 'station'), may hold values from -6 to 6
- value_states: bfloat16 [8, 64, 128, 768], P('dp', 'station'), may hold values from -15 to 15
- grad_output: bfloat16 [8, 64, 128, 768], P('dp', 'station'), may hold values from -6 to 6
- out_weight: bfloat16 [768, 768], replicated, may hold values from -0.21875 to 0.21875
- partner_ids: int32 [64, 6], replicated, may hold values from 0 to 63, as said below
- partner_count: int32 [64], replicated, may hold values from 1 to 6, as said below
Outputs:
- layer_output: bfloat16 [8, 64, 128, 768], P('dp', 'station')
- grad_query: bfloat16 [8, 64, 128, 768], P('dp', 'station')
- grad_key: bfloat16 [8, 64, 128, 768], P('dp', 'station')
- grad_value: bfloat16 [8, 64, 128, 768], P('dp', 'station')
- grad_weight: float32 [768, 768], P('dp')
The draws below stay inside these ranges and needn't reach their ends.
Inputs may be any that keep to these rules, and one draw needn't show every extreme that they name: `partner_ids`: row s lists 6 different stations other than s, all held by devices within 3 places of the device of s along the station axis, taken as a loop (station s lies on device s); only the first partner_count[s] entries are partners. `partner_count`: some station has exactly 6 partners.
All inputs are finite; a program needn't handle non-finite values.
Results may differ from the reference program's by a relative error of at most 0.025.
Values may be sent and summed in bfloat16 or wider, within the bound.
A program may use at most 64 MiB of HBM per device.

```python
import math
import jax
import jax.numpy as jnp
from jax import lax

D = 768
HEADS = 12
SPAN = 128
PMAX = 6
HOPS = 3
STA_DEV = 1
STATIONS = 64
WINDOWS = 8


def draw_query_states(key, part):
    shape = (WINDOWS, STATIONS, SPAN, D)
    result = jnp.clip(jax.random.normal(jax.random.fold_in(key, 1), shape, jnp.float32), -6.0, 6.0)
    return result.astype(jnp.bfloat16)


def draw_key_states(key, part):
    shape = (WINDOWS, STATIONS, SPAN, D)
    result = jnp.clip(jax.random.normal(jax.random.fold_in(key, 2), shape, jnp.float32), -6.0, 6.0)
    return result.astype(jnp.bfloat16)


def draw_partner_count(key, part):
    order = jax.random.permutation(jax.random.fold_in(key, 3), STATIONS)
    base_count = jax.random.randint(jax.random.fold_in(key, 4), (STATIONS,), 1, 3)
    return jnp.where(order < max(1, STATIONS // 16), PMAX, base_count).astype(jnp.int32)


def draw_partner_ids(key, part):
    others = (2 * HOPS + 1) * STA_DEV - 1
    ranking = jax.random.randint(jax.random.fold_in(key, 6), (STATIONS, others), 0, 1 << 18) * 64 + jnp.arange(others, dtype=jnp.int32)[None, :]
    unused, picks = lax.top_k(ranking, PMAX)
    station_ids = jnp.arange(STATIONS, dtype=jnp.int32)[:, None]
    self_pos = HOPS * STA_DEV + station_ids % STA_DEV
    window_pos = picks + (picks >= self_pos).astype(jnp.int32)
    global_ids = jnp.mod(station_ids // STA_DEV * STA_DEV - HOPS * STA_DEV + window_pos, STATIONS)
    return global_ids.astype(jnp.int32)


def level_of(key, extent, split, least, top_value):
    gain, own = 1.0, jax.random.fold_in(key, 6)
    for dim, blocks in split:
        draws = jnp.exp(jax.random.uniform(jax.random.fold_in(own, dim), (blocks,), jnp.float32, least / len(split), top_value / len(split)))
        gain = gain * jnp.repeat(draws, extent[dim] // blocks).reshape([-1 if axis == dim else 1 for axis in range(len(extent))])
    return gain


def scatter_about(key, extent, width, limit, pieces=(), kind=jnp.bfloat16):
    array = width * jax.random.normal(key, extent, jnp.float32)
    if pieces:
        array = array * level_of(key, extent, pieces, -0.22, 0.18)
    return jnp.clip(array, -limit, limit).astype(kind)


def setup_inputs(seed: int = 0) -> dict:
    keys = jax.random.split(jax.random.key(seed), 8)
    return {
        "query_states": draw_query_states(jax.random.fold_in(keys[7], 71), 0),
        "key_states": draw_key_states(jax.random.fold_in(keys[7], 71), 0),
        "value_states": scatter_about(keys[2], (WINDOWS, STATIONS, SPAN, D), 2.5, 15.0, ((0, 8), (1, 64))),
        "grad_output": scatter_about(keys[3], (WINDOWS, STATIONS, SPAN, D), 1.0, 6.0, ((0, 8), (1, 64))),
        "out_weight": scatter_about(keys[4], (D, D), D ** -0.5, 0.21875),
        "partner_ids": draw_partner_ids(jax.random.fold_in(keys[7], 71), 0),
        "partner_count": draw_partner_count(jax.random.fold_in(keys[7], 71), 0),
    }


neg_big = -1e+30

def reference(query_states, key_states, value_states, grad_output, out_weight, partner_ids, partner_count):
    window_count, station_count, span_rows, model_width = query_states.shape
    head_count = HEADS
    head_width = model_width // head_count
    score_scale = 1.0 / math.sqrt(head_width)
    slot_count = PMAX + 1
    row_count = window_count * station_count * span_rows
    flat_grad = grad_output.reshape(row_count, model_width)
    grad_mixed = jnp.dot(flat_grad, out_weight.T, preferred_element_type=jnp.float32).astype(jnp.bfloat16)
    grad_mixed = grad_mixed.reshape(query_states.shape)

    def visit(carry, number):
        key_acc, value_acc = carry
        window_no = number // station_count
        station_no = number % station_count
        slot_station = jnp.concatenate([station_no[None].astype(jnp.int32), partner_ids[station_no].astype(jnp.int32)])
        slot_live = (jnp.arange(slot_count, dtype=jnp.int32) <= partner_count[station_no]).astype(jnp.float32)
        allowed = jnp.repeat(slot_live, span_rows)
        key_rows = key_states[window_no][slot_station].astype(jnp.float32).reshape(slot_count * span_rows, head_count, head_width)
        value_rows = value_states[window_no][slot_station].astype(jnp.float32).reshape(slot_count * span_rows, head_count, head_width)
        query_rows = query_states[window_no, station_no].astype(jnp.float32).reshape(span_rows, head_count, head_width)
        grad_rows = grad_mixed[window_no, station_no].astype(jnp.float32).reshape(span_rows, head_count, head_width)
        scores = jnp.einsum('qhd,khd->hqk', query_rows, key_rows) * score_scale
        masked = jnp.where(allowed[None, None, :] > 0, scores, neg_big)
        row_max = lax.optimization_barrier(jnp.max(masked, -1))
        weights_raw = jnp.exp(masked - row_max[..., None])
        row_sum = lax.optimization_barrier(jnp.sum(weights_raw, -1))
        attn_probs = weights_raw / row_sum[..., None]
        probs_half = lax.optimization_barrier(attn_probs.astype(jnp.bfloat16)).astype(jnp.float32)
        mixed_rows = jnp.einsum('hqk,khd->qhd', probs_half, value_rows).astype(jnp.bfloat16)
        mixed_back = lax.optimization_barrier(mixed_rows).astype(jnp.float32)
        row_delta = lax.optimization_barrier(jnp.sum(grad_rows * mixed_back, -1)).T
        grad_probs = jnp.einsum('qhd,khd->hqk', grad_rows, value_rows)
        grad_scores = (attn_probs * (grad_probs - row_delta[..., None])).astype(jnp.bfloat16)
        scores_back = lax.optimization_barrier(grad_scores).astype(jnp.float32)
        query_grad = (score_scale * jnp.einsum('hqk,khd->qhd', scores_back, key_rows)).astype(jnp.bfloat16)
        key_part = score_scale * jnp.einsum('hqk,qhd->khd', scores_back, query_rows)
        value_part = jnp.einsum('hqk,qhd->khd', probs_half, grad_rows)
        key_acc = key_acc.at[window_no, slot_station].add(key_part.reshape(slot_count, span_rows, model_width))
        value_acc = value_acc.at[window_no, slot_station].add(value_part.reshape(slot_count, span_rows, model_width))
        return ((key_acc, value_acc), (mixed_rows.reshape(span_rows, model_width), query_grad.reshape(span_rows, model_width)))
    zeros = jnp.zeros(key_states.shape, jnp.float32)
    numbers = jnp.arange(window_count * station_count, dtype=jnp.int32)
    (key_acc, value_acc), (mixed_all, query_all) = lax.scan(visit, (zeros, zeros), numbers)
    mixed_flat = mixed_all.reshape(row_count, model_width)
    layer_output = jnp.dot(mixed_flat, out_weight, preferred_element_type=jnp.float32).astype(jnp.bfloat16)
    grad_weight = jnp.dot(mixed_flat.T, flat_grad, preferred_element_type=jnp.float32) / math.sqrt(row_count)
    return (layer_output.reshape(query_states.shape), query_all.reshape(query_states.shape), key_acc.astype(jnp.bfloat16), value_acc.astype(jnp.bfloat16), grad_weight)
```

```python
import math

import jax
import jax.numpy as jnp
from jax import lax
from jax.experimental import pallas as pl
from jax.experimental.pallas import tpu as pltpu
from jax.sharding import PartitionSpec as P

HEADS = 12
PMAX = 6
HOPS = 3
SPAN = 128
D = 768
PAIRS = HEADS // 2
STATIONS = 64
ZDIM = 16
XDIM = 4
YDIM = 4
GROUP = 4
DP = 8
ROWS = D // DP
MESH = pl.DeviceIdType.MESH
BF = jnp.bfloat16
F32 = jnp.float32
dead_bias = -1e30
KEY, VALUE, GRAD, QUERY = 0, 1, 2, 3


def dot(a, b, ca=1, cb=0):
    return lax.dot_general(a, b, (((ca,), (cb,)), ((), ())), preferred_element_type=F32)


def kernel(
    ids, cnt, q_ref, k_ref, v_ref, g_ref, w_ref,
    lo_ref, dq_ref, dk_ref, dv_ref, gw_ref,
    gat, kt, vt, s_buf, bdq, bdm, mixed_t, dq_t, stat, acc_k, acc_v,
    gwp, w1r, w2s, w2r, xs, xr, z1s, z1r, z2s, z2r, fin, xfin,
    send, recv,
):
    dp = lax.axis_index("dp")
    me = lax.axis_index("station")
    y, core = dp // 2, dp % 2
    x, z = me // ZDIM, me % ZDIM
    za, zb = z // GROUP, z % GROUP

    def station(offset):
        return (dp, lax.rem(me + offset + STATIONS, STATIONS))

    core_peer = (y * 2 + (1 - core), me)
    y_peers = [(lax.rem(y + o, YDIM) * 2 + core, me) for o in (1, 2, 3)]
    x_peers = [(dp, lax.rem(x + o, XDIM) * ZDIM + z) for o in (1, 2, 3)]
    zb_peers = [(dp, x * ZDIM + za * GROUP + lax.rem(zb + o, GROUP)) for o in (1, 2, 3)]
    za_peers = [(dp, x * ZDIM + lax.rem(za + o, GROUP) * GROUP + zb) for o in (1, 2, 3)]
    near = [station(o) for o in (1, 2, 3, -1, -2, -3)]
    greet = [core_peer] + y_peers + x_peers + zb_peers + za_peers + near
    barrier = pltpu.get_barrier_semaphore()
    for peer in greet:
        pl.semaphore_signal(barrier, inc=1, device_id=peer, device_id_type=MESH)
    pl.semaphore_wait(barrier, len(greet))

    started = []

    def remote(src, dst, number, peer):
        copy = pltpu.make_async_remote_copy(
            src_ref=src, dst_ref=dst, send_sem=send.at[number], recv_sem=recv.at[number],
            device_id=peer, device_id_type=MESH,
        )
        copy.start()
        started.append(copy)
        return copy

    own = (k_ref, v_ref, g_ref, q_ref)
    flights = {}

    def hop(item, h):
        for way in (0, 1):
            src = own[item] if h == 1 else gat.at[item, way, h - 2]
            flights[item, way, h] = remote(
                src, gat.at[item, way, h - 1], (item * 2 + way) * 3 + h - 1,
                station(1 if way == 0 else -1),
            )

    def arrived(item, h):
        for way in (0, 1):
            flights[item, way, h].wait_recv()

    def block(item, j):
        if j == 0:
            return own[item]
        return gat.at[item, (j - 1) // 3, (j - 1) % 3]

    hop(KEY, 1)
    hop(VALUE, 1)

    offsets = (0, -1, -2, -3, 1, 2, 3)

    def listed(reader, block_station):
        hit = jnp.int32(0)
        for p in range(PMAX):
            same = ids[reader, p] == block_station
            live = p < cnt[reader]
            hit = hit + jnp.where(same & live, jnp.int32(1), jnp.int32(0))
        return jnp.where(hit > 0, F32(0.0), F32(dead_bias))

    bias_f, bias_b = [F32(0.0)], [F32(0.0)]
    for o in offsets[1:]:
        other = station(o)[1]
        bias_f.append(listed(me, other))
        bias_b.append(listed(other, me))

    bdq[...] = jnp.zeros_like(bdq)
    bdm[...] = jnp.zeros_like(bdm)

    def prepare(j, slot):
        q_t = block(QUERY, j)[...].T
        q_t = (q_t.astype(F32) * 0.125).astype(BF)
        m_t = dot(w_ref[...], block(GRAD, j)[...], 1, 1).astype(BF)
        for p in range(PAIRS):
            a, b = p * 128, p * 128 + 64
            bdq[slot, p, 0:64, 0:128] = q_t[a : a + 64]
            bdq[slot, p, 64:128, 128:256] = q_t[b : b + 64]
            bdm[slot, p, 0:64, 0:128] = m_t[a : a + 64]
            bdm[slot, p, 64:128, 128:256] = m_t[b : b + 64]

    def turn(j):
        kt[j] = block(KEY, j)[...].T
        vt[j] = block(VALUE, j)[...].T

    prepare(0, 0)
    turn(0)
    for h in (1, 2):
        for item in (KEY, VALUE):
            arrived(item, h)
            hop(item, h + 1)
        if h == 2:
            hop(GRAD, 1)
            hop(QUERY, 1)
        turn(h)
        turn(3 + h)
    arrived(KEY, 3)
    arrived(VALUE, 3)
    turn(3)
    turn(6)

    def forward(p, carry):
        cols = pl.ds(pl.multiple_of(p * 128, 128), 128)
        rhs_q, rhs_m = bdq[0, p], bdm[0, p]
        top = None
        for j in range(7):
            s = dot(block(KEY, j)[:, cols], rhs_q) + bias_f[j]
            s_buf[j] = s
            m = jnp.max(s, 0, keepdims=True)
            top = m if top is None else jnp.maximum(top, m)
        total = jnp.zeros_like(top)
        for j in range(7):
            e = jnp.exp(s_buf[j] - top)
            s_buf[j] = e
            total = total + jnp.sum(e, 0, keepdims=True)
        inv = 1.0 / total
        out = jnp.zeros((128, 256), F32)
        for j in range(7):
            prob = s_buf[j] * inv
            s_buf[j] = prob
            out = out + dot(vt[j, cols, :], prob.astype(BF))
        out = out.astype(BF)
        mixed_t[pl.ds(pl.multiple_of(p * 128, 128), 64), :] = out[0:64, 0:128]
        mixed_t[pl.ds(pl.multiple_of(p * 128 + 64, 64), 64), :] = out[64:128, 128:256]
        delta = jnp.sum(rhs_m.astype(F32) * out.astype(F32), 0, keepdims=True)
        stat[0, pl.ds(p, 1), :] = top + jnp.log(total)
        stat[0, pl.ds(p + 8, 1), :] = delta
        grad = jnp.zeros((128, 256), F32)
        for j in range(7):
            d_prob = dot(block(VALUE, j)[:, cols], rhs_m)
            d_score = (s_buf[j] * (d_prob - delta)).astype(BF)
            grad = grad + dot(kt[j, cols, :], d_score)
        grad = (grad * 0.125).astype(BF)
        dq_t[pl.ds(pl.multiple_of(p * 128, 128), 64), :] = grad[0:64, 0:128]
        dq_t[pl.ds(pl.multiple_of(p * 128 + 64, 64), 64), :] = grad[64:128, 128:256]
        return carry

    lax.fori_loop(0, 4, forward, 0)
    arrived(GRAD, 1)
    hop(GRAD, 2)
    lax.fori_loop(4, PAIRS, forward, 0)

    for d in range(DP):
        rows = mixed_t[d * ROWS : (d + 1) * ROWS, :]
        gwp[d % 2, d // 2] = dot(rows, g_ref[...]).astype(BF)
    stats = []
    for d in (1, 2, 3):
        stats.append(remote(stat.at[0], stat.at[d], 24 + d - 1, station(d)))
        stats.append(remote(stat.at[0], stat.at[3 + d], 27 + d - 1, station(-d)))
    core_copy = remote(gwp.at[1 - core], w1r, 30, core_peer)
    arrived(QUERY, 1)
    hop(QUERY, 2)
    lo_ref[...] = dot(mixed_t[...].T, w_ref[...]).astype(BF)
    dq_ref[...] = dq_t[...].T

    core_copy.wait_recv()
    for n in range(YDIM):
        w2s[n] = (gwp[core, n].astype(F32) + w1r[n].astype(F32)).astype(BF)
    y_copies = [
        remote(w2s.at[lax.rem(y + o, YDIM)], w2r.at[o - 1], 31 + o - 1, y_peers[o - 1])
        for o in (1, 2, 3)
    ]

    acc_k[...] = jnp.zeros_like(acc_k)
    acc_v[...] = jnp.zeros_like(acc_v)

    def backward(j, slot):
        def step(p, carry):
            cols = pl.ds(pl.multiple_of(p * 128, 128), 128)
            rhs_q, rhs_m = bdq[slot, p], bdm[slot, p]
            shift = bias_b[j] - stat[j, pl.ds(p, 1), :]
            prob = jnp.exp(dot(k_ref[:, cols], rhs_q) + shift)
            d_prob = dot(v_ref[:, cols], rhs_m)
            d_score = (prob * (d_prob - stat[j, pl.ds(p + 8, 1), :])).astype(BF)
            acc_v[:, cols] += dot(prob.astype(BF), rhs_m, 1, 1)
            acc_k[:, cols] += dot(d_score, rhs_q, 1, 1)
            return carry

        lax.fori_loop(0, PAIRS, step, 0)

    backward(0, 0)
    arrived(GRAD, 2)
    hop(GRAD, 3)
    for copy in stats:
        copy.wait_recv()
    prepare(1, 1)
    backward(1, 1)
    arrived(QUERY, 2)
    hop(QUERY, 3)
    prepare(4, 0)
    backward(4, 0)

    for copy in y_copies:
        copy.wait_recv()
    total = w2s[y].astype(F32)
    for n in range(3):
        total = total + w2r[n].astype(F32)
    for n in range(XDIM):
        for r in range(3):
            lower = n * 24 + r * 8
            piece = total[lower : lower + 8]
            xs[n, r] = jnp.concatenate([piece[:, 0:384], piece[:, 384:768]], 0).astype(BF)
    x_copies = [
        remote(xs.at[lax.rem(x + o, XDIM)], xr.at[o - 1], 34 + o - 1, x_peers[o - 1])
        for o in (1, 2, 3)
    ]
    prepare(2, 1)
    backward(2, 1)

    for copy in x_copies:
        copy.wait_recv()
    part = xs[x].astype(F32)
    for n in range(3):
        part = part + xr[n].astype(F32)
    z1s[0:3] = part.astype(BF)
    z1s[3] = jnp.zeros_like(z1s[3])
    zb_copies = [
        remote(z1s.at[lax.rem(zb + o, GROUP)], z1r.at[o - 1], 37 + o - 1, zb_peers[o - 1])
        for o in (1, 2, 3)
    ]
    prepare(5, 0)
    backward(5, 0)

    for copy in zb_copies:
        copy.wait_recv()
    part = z1s[zb].astype(F32)
    for n in range(3):
        part = part + z1r[n].astype(F32)
    z2s[...] = part.astype(BF)
    za_copies = [remote(z2s, z2r.at[o - 1], 40 + o - 1, za_peers[o - 1]) for o in (1, 2, 3)]

    arrived(GRAD, 3)
    arrived(QUERY, 3)
    prepare(3, 1)
    backward(3, 1)
    prepare(6, 0)
    backward(6, 0)
    dk_ref[...] = acc_k[...].astype(BF)
    dv_ref[...] = acc_v[...].astype(BF)

    for copy in za_copies:
        copy.wait_recv()
    part = z2s[...].astype(F32)
    for n in range(3):
        part = part + z2r[n].astype(F32)
    fin[zb] = (part * (1.0 / math.sqrt(DP * STATIONS * SPAN))).astype(BF)
    zb_copies = [remote(fin.at[zb], fin.at[zb], 43 + o - 1, zb_peers[o - 1]) for o in (1, 2, 3)]
    for copy in zb_copies:
        copy.wait_recv()
    x_copies = [
        remote(fin.at[pl.ds(0, 3)], xfin.at[x], 46 + o - 1, x_peers[o - 1]) for o in (1, 2, 3)
    ]
    xfin[x] = fin[0:3]
    for copy in x_copies:
        copy.wait_recv()
    for n in range(XDIM):
        for r in range(3):
            lower = n * 24 + r * 8
            piece = xfin[n, r].astype(F32)
            gw_ref[lower : lower + 8, 0:384] = piece[0:8]
            gw_ref[lower : lower + 8, 384:768] = piece[8:16]
    for copy in started:
        copy.wait_send()


def local(
    query_states, key_states, value_states, grad_output, out_weight, partner_ids, partner_count
):
    shape = query_states.shape
    flat = [a.reshape(SPAN, D) for a in (query_states, key_states, value_states, grad_output)]
    vmem = pl.BlockSpec(memory_space=pltpu.VMEM)
    smem = pl.BlockSpec(memory_space=pltpu.SMEM)
    rows = jax.ShapeDtypeStruct((SPAN, D), BF)
    copies = 49
    outs = pl.pallas_call(
        kernel,
        out_shape=(rows, rows, rows, rows, jax.ShapeDtypeStruct((ROWS, D), F32)),
        in_specs=[smem, smem] + [vmem] * 5,
        out_specs=(vmem,) * 5,
        scratch_shapes=[
            pltpu.VMEM((4, 2, HOPS, SPAN, D), BF),
            pltpu.VMEM((7, D, SPAN), BF),
            pltpu.VMEM((7, D, SPAN), BF),
            pltpu.VMEM((7, SPAN, 256), F32),
            pltpu.VMEM((2, PAIRS, 128, 256), BF),
            pltpu.VMEM((2, PAIRS, 128, 256), BF),
            pltpu.VMEM((D, SPAN), BF),
            pltpu.VMEM((D, SPAN), BF),
            pltpu.VMEM((7, 16, 256), F32),
            pltpu.VMEM((SPAN, D), F32),
            pltpu.VMEM((SPAN, D), F32),
            pltpu.VMEM((2, YDIM, ROWS, D), BF),
            pltpu.VMEM((YDIM, ROWS, D), BF),
            pltpu.VMEM((YDIM, ROWS, D), BF),
            pltpu.VMEM((3, ROWS, D), BF),
            pltpu.VMEM((XDIM, 3, 16, 384), BF),
            pltpu.VMEM((3, 3, 16, 384), BF),
            pltpu.VMEM((GROUP, 16, 384), BF),
            pltpu.VMEM((3, 16, 384), BF),
            pltpu.VMEM((16, 384), BF),
            pltpu.VMEM((3, 16, 384), BF),
            pltpu.VMEM((GROUP, 16, 384), BF),
            pltpu.VMEM((XDIM, 3, 16, 384), BF),
            pltpu.SemaphoreType.DMA((copies,)),
            pltpu.SemaphoreType.DMA((copies,)),
        ],
        compiler_params=pltpu.CompilerParams(
            collective_id=0, has_side_effects=True, vmem_limit_bytes=48 * 1024 * 1024
        ),
    )(partner_ids, partner_count, *flat, out_weight)
    return tuple(a.reshape(shape) for a in outs[:4]) + (outs[4],)


def solution(mesh):
    tokens = P("dp", "station", None, None)
    return jax.shard_map(
        local,
        mesh=mesh,
        in_specs=(tokens,) * 4 + (P(), P(), P()),
        out_specs=(tokens,) * 4 + (P("dp", None),),
        check_vma=False,
    )
```

```python
import math

import jax
import jax.numpy as jnp
from jax import lax
from jax.experimental import pallas as pl
from jax.experimental.pallas import tpu as pltpu
from jax.sharding import PartitionSpec as P

HEADS = 12
PMAX = 6
HOPS = 3
SPAN = 128
D = 768
PAIRS = HEADS // 2
STATIONS = 64
ZDIM = 16
XDIM = 4
YDIM = 4
GROUP = 4
DP = 8
ROWS = D // DP
MESH = pl.DeviceIdType.MESH
BF = jnp.bfloat16
F32 = jnp.float32
dead_bias = -1e30
KEY, VALUE, GRAD, QUERY = 0, 1, 2, 3


def dot(a, b, ca=1, cb=0):
    return lax.dot_general(a, b, (((ca,), (cb,)), ((), ())), preferred_element_type=F32)


def kernel(
    ids, cnt, q_in, k_in, v_in, g_in, w_in,
    lo_out, dq_out, dk_out, dv_out, gw_out,
    gat, kt, vt, s_buf, bdq, bdm, mixed_t, dq_t, stat, acc_k, acc_v,
    gwp, w1r, w2s, w2r, xs, xr, z1s, z1r, z2s, z2r, fin, xfin,
    q_ref, k_ref, v_ref, g_ref, w_ref,
    lo_ref, dq_ref, dk_ref, dv_ref, gw_ref, load, put, send, recv,
):
    loads = [
        pltpu.make_async_copy(src, dst, load.at[n])
        for n, (src, dst) in enumerate(
            ((w_in, w_ref), (g_in, g_ref), (q_in, q_ref), (k_in, k_ref), (v_in, v_ref))
        )
    ]
    for copy in loads:
        copy.start()
    dp = lax.axis_index("dp")
    me = lax.axis_index("station")
    y, core = dp // 2, dp % 2
    x, z = me // ZDIM, me % ZDIM
    za, zb = z // GROUP, z % GROUP

    def station(offset):
        return (dp, lax.rem(me + offset + STATIONS, STATIONS))

    core_peer = (y * 2 + (1 - core), me)
    y_peers = [(lax.rem(y + o, YDIM) * 2 + core, me) for o in (1, 2, 3)]
    x_peers = [(dp, lax.rem(x + o, XDIM) * ZDIM + z) for o in (1, 2, 3)]
    zb_peers = [(dp, x * ZDIM + za * GROUP + lax.rem(zb + o, GROUP)) for o in (1, 2, 3)]
    za_peers = [(dp, x * ZDIM + lax.rem(za + o, GROUP) * GROUP + zb) for o in (1, 2, 3)]
    near = [station(o) for o in (1, 2, 3, -1, -2, -3)]
    greet = [core_peer] + y_peers + x_peers + zb_peers + za_peers + near
    barrier = pltpu.get_barrier_semaphore()
    for peer in greet:
        pl.semaphore_signal(barrier, inc=1, device_id=peer, device_id_type=MESH)
    pl.semaphore_wait(barrier, len(greet))

    started = []

    def remote(src, dst, number, peer):
        copy = pltpu.make_async_remote_copy(
            src_ref=src, dst_ref=dst, send_sem=send.at[number], recv_sem=recv.at[number],
            device_id=peer, device_id_type=MESH,
        )
        copy.start()
        started.append(copy)
        return copy

    source = (k_in, v_in, g_in, q_in)
    own = (k_ref, v_ref, g_ref, q_ref)
    flights = {}
    puts = []

    def store(n, src, dst):
        copy = pltpu.make_async_copy(src, dst, put.at[n])
        copy.start()
        puts.append(copy)

    def hop(item, h):
        for way in (0, 1):
            src = source[item] if h == 1 else gat.at[item, way, h - 2]
            flights[item, way, h] = remote(
                src, gat.at[item, way, h - 1], (item * 2 + way) * 3 + h - 1,
                station(1 if way == 0 else -1),
            )

    def arrived(item, h):
        for way in (0, 1):
            flights[item, way, h].wait_recv()

    def block(item, j):
        if j == 0:
            return own[item]
        return gat.at[item, (j - 1) // 3, (j - 1) % 3]

    hop(KEY, 1)
    hop(VALUE, 1)

    offsets = (0, -1, -2, -3, 1, 2, 3)

    def listed(reader, block_station):
        hit = jnp.int32(0)
        for p in range(PMAX):
            same = ids[reader, p] == block_station
            live = p < cnt[reader]
            hit = hit + jnp.where(same & live, jnp.int32(1), jnp.int32(0))
        return jnp.where(hit > 0, F32(0.0), F32(dead_bias))

    bias_f, bias_b = [F32(0.0)], [F32(0.0)]
    for o in offsets[1:]:
        other = station(o)[1]
        bias_f.append(listed(me, other))
        bias_b.append(listed(other, me))

    bdq[...] = jnp.zeros_like(bdq)
    bdm[...] = jnp.zeros_like(bdm)
    for copy in loads:
        copy.wait()

    def prepare(j, slot):
        q_t = block(QUERY, j)[...].T
        q_t = (q_t.astype(F32) * 0.125).astype(BF)
        m_t = dot(w_ref[...], block(GRAD, j)[...], 1, 1).astype(BF)
        for p in range(PAIRS):
            a, b = p * 128, p * 128 + 64
            bdq[slot, p, 0:64, 0:128] = q_t[a : a + 64]
            bdq[slot, p, 64:128, 128:256] = q_t[b : b + 64]
            bdm[slot, p, 0:64, 0:128] = m_t[a : a + 64]
            bdm[slot, p, 64:128, 128:256] = m_t[b : b + 64]

    def turn(j):
        kt[j] = block(KEY, j)[...].T
        vt[j] = block(VALUE, j)[...].T

    prepare(0, 0)
    turn(0)
    for h in (1, 2):
        for item in (KEY, VALUE):
            arrived(item, h)
            hop(item, h + 1)
        if h == 2:
            hop(GRAD, 1)
            hop(QUERY, 1)
        turn(h)
        turn(3 + h)
    arrived(KEY, 3)
    arrived(VALUE, 3)
    turn(3)
    turn(6)

    def forward(p, carry):
        cols = pl.ds(pl.multiple_of(p * 128, 128), 128)
        rhs_q, rhs_m = bdq[0, p], bdm[0, p]
        top = None
        for j in range(7):
            s = dot(block(KEY, j)[:, cols], rhs_q) + bias_f[j]
            s_buf[j] = s
            m = jnp.max(s, 0, keepdims=True)
            top = m if top is None else jnp.maximum(top, m)
        total = jnp.zeros_like(top)
        for j in range(7):
            e = jnp.exp(s_buf[j] - top)
            s_buf[j] = e
            total = total + jnp.sum(e, 0, keepdims=True)
        inv = 1.0 / total
        out = jnp.zeros((128, 256), F32)
        for j in range(7):
            prob = s_buf[j] * inv
            s_buf[j] = prob
            out = out + dot(vt[j, cols, :], prob.astype(BF))
        out = out.astype(BF)
        mixed_t[pl.ds(pl.multiple_of(p * 128, 128), 64), :] = out[0:64, 0:128]
        mixed_t[pl.ds(pl.multiple_of(p * 128 + 64, 64), 64), :] = out[64:128, 128:256]
        delta = jnp.sum(rhs_m.astype(F32) * out.astype(F32), 0, keepdims=True)
        stat[0, pl.ds(p, 1), :] = top + jnp.log(total)
        stat[0, pl.ds(p + 8, 1), :] = delta
        grad = jnp.zeros((128, 256), F32)
        for j in range(7):
            d_prob = dot(block(VALUE, j)[:, cols], rhs_m)
            d_score = (s_buf[j] * (d_prob - delta)).astype(BF)
            grad = grad + dot(kt[j, cols, :], d_score)
        grad = (grad * 0.125).astype(BF)
        dq_t[pl.ds(pl.multiple_of(p * 128, 128), 64), :] = grad[0:64, 0:128]
        dq_t[pl.ds(pl.multiple_of(p * 128 + 64, 64), 64), :] = grad[64:128, 128:256]
        return carry

    lax.fori_loop(0, 4, forward, 0)
    arrived(GRAD, 1)
    hop(GRAD, 2)
    lax.fori_loop(4, PAIRS, forward, 0)

    for d in range(DP):
        rows = mixed_t[d * ROWS : (d + 1) * ROWS, :]
        gwp[d % 2, d // 2] = dot(rows, g_ref[...]).astype(BF)
    core_copy = remote(gwp.at[1 - core], w1r, 30, core_peer)
    stats = []
    for d in (1, 2, 3):
        stats.append(remote(stat.at[0], stat.at[d], 24 + d - 1, station(d)))
        stats.append(remote(stat.at[0], stat.at[3 + d], 27 + d - 1, station(-d)))
    arrived(QUERY, 1)
    hop(QUERY, 2)
    lo_ref[...] = dot(mixed_t[...].T, w_ref[...]).astype(BF)
    store(0, lo_ref, lo_out)

    core_copy.wait_recv()
    for n in range(YDIM):
        w2s[n] = (gwp[core, n].astype(F32) + w1r[n].astype(F32)).astype(BF)
    y_copies = [
        remote(w2s.at[lax.rem(y + o, YDIM)], w2r.at[o - 1], 31 + o - 1, y_peers[o - 1])
        for o in (1, 2, 3)
    ]

    dq_ref[...] = dq_t[...].T
    store(1, dq_ref, dq_out)
    acc_k[...] = jnp.zeros_like(acc_k)
    acc_v[...] = jnp.zeros_like(acc_v)

    def backward(j, slot):
        def step(p, carry):
            cols = pl.ds(pl.multiple_of(p * 128, 128), 128)
            rhs_q, rhs_m = bdq[slot, p], bdm[slot, p]
            shift = bias_b[j] - stat[j, pl.ds(p, 1), :]
            prob = jnp.exp(dot(k_ref[:, cols], rhs_q) + shift)
            d_prob = dot(v_ref[:, cols], rhs_m)
            d_score = (prob * (d_prob - stat[j, pl.ds(p + 8, 1), :])).astype(BF)
            acc_v[:, cols] += dot(prob.astype(BF), rhs_m, 1, 1)
            acc_k[:, cols] += dot(d_score, rhs_q, 1, 1)
            return carry

        lax.fori_loop(0, PAIRS, step, 0)

    backward(0, 0)
    arrived(GRAD, 2)
    hop(GRAD, 3)
    for copy in stats:
        copy.wait_recv()
    prepare(1, 1)
    backward(1, 1)
    arrived(QUERY, 2)
    hop(QUERY, 3)
    prepare(4, 0)
    backward(4, 0)

    for copy in y_copies:
        copy.wait_recv()
    total = w2s[y].astype(F32)
    for n in range(3):
        total = total + w2r[n].astype(F32)
    for n in range(XDIM):
        for r in range(3):
            lower = n * 24 + r * 8
            piece = total[lower : lower + 8]
            xs[n, r] = jnp.concatenate([piece[:, 0:384], piece[:, 384:768]], 0).astype(BF)
    x_copies = [
        remote(xs.at[lax.rem(x + o, XDIM)], xr.at[o - 1], 34 + o - 1, x_peers[o - 1])
        for o in (1, 2, 3)
    ]
    prepare(2, 1)
    backward(2, 1)

    for copy in x_copies:
        copy.wait_recv()
    part = xs[x].astype(F32)
    for n in range(3):
        part = part + xr[n].astype(F32)
    z1s[0:3] = part.astype(BF)
    z1s[3] = jnp.zeros_like(z1s[3])
    zb_copies = [
        remote(z1s.at[lax.rem(zb + o, GROUP)], z1r.at[o - 1], 37 + o - 1, zb_peers[o - 1])
        for o in (1, 2, 3)
    ]
    prepare(5, 0)
    backward(5, 0)

    for copy in zb_copies:
        copy.wait_recv()
    part = z1s[zb].astype(F32)
    for n in range(3):
        part = part + z1r[n].astype(F32)
    z2s[...] = part.astype(BF)
    za_copies = [remote(z2s, z2r.at[o - 1], 40 + o - 1, za_peers[o - 1]) for o in (1, 2, 3)]

    arrived(GRAD, 3)
    arrived(QUERY, 3)
    prepare(3, 1)
    backward(3, 1)
    prepare(6, 0)
    backward(6, 0)
    dk_ref[...] = acc_k[...].astype(BF)
    dv_ref[...] = acc_v[...].astype(BF)
    store(2, dk_ref, dk_out)
    store(3, dv_ref, dv_out)

    for copy in za_copies:
        copy.wait_recv()
    part = z2s[...].astype(F32)
    for n in range(3):
        part = part + z2r[n].astype(F32)
    fin[zb] = (part * (1.0 / math.sqrt(DP * STATIONS * SPAN))).astype(BF)
    zb_copies = [remote(fin.at[zb], fin.at[zb], 43 + o - 1, zb_peers[o - 1]) for o in (1, 2, 3)]
    for copy in zb_copies:
        copy.wait_recv()
    x_copies = [
        remote(fin.at[pl.ds(0, 3)], xfin.at[x], 46 + o - 1, x_peers[o - 1]) for o in (1, 2, 3)
    ]
    xfin[x] = fin[0:3]
    for copy in x_copies:
        copy.wait_recv()
    for n in range(XDIM):
        for r in range(3):
            lower = n * 24 + r * 8
            piece = xfin[n, r].astype(F32)
            gw_ref[lower : lower + 8, 0:384] = piece[0:8]
            gw_ref[lower : lower + 8, 384:768] = piece[8:16]
    store(4, gw_ref, gw_out)
    for copy in started:
        copy.wait_send()
    for copy in puts:
        copy.wait()


def local(
    query_states, key_states, value_states, grad_output, out_weight, partner_ids, partner_count
):
    shape = query_states.shape
    flat = [a.reshape(SPAN, D) for a in (query_states, key_states, value_states, grad_output)]
    hbm = pl.BlockSpec(memory_space=pl.ANY)
    smem = pl.BlockSpec(memory_space=pltpu.SMEM)
    rows = jax.ShapeDtypeStruct((SPAN, D), BF)
    copies = 49
    outs = pl.pallas_call(
        kernel,
        out_shape=(rows, rows, rows, rows, jax.ShapeDtypeStruct((ROWS, D), F32)),
        in_specs=[smem, smem] + [hbm] * 5,
        out_specs=(hbm,) * 5,
        scratch_shapes=[
            pltpu.VMEM((4, 2, HOPS, SPAN, D), BF),
            pltpu.VMEM((7, D, SPAN), BF),
            pltpu.VMEM((7, D, SPAN), BF),
            pltpu.VMEM((7, SPAN, 256), F32),
            pltpu.VMEM((2, PAIRS, 128, 256), BF),
            pltpu.VMEM((2, PAIRS, 128, 256), BF),
            pltpu.VMEM((D, SPAN), BF),
            pltpu.VMEM((D, SPAN), BF),
            pltpu.VMEM((7, 16, 256), F32),
            pltpu.VMEM((SPAN, D), F32),
            pltpu.VMEM((SPAN, D), F32),
            pltpu.VMEM((2, YDIM, ROWS, D), BF),
            pltpu.VMEM((YDIM, ROWS, D), BF),
            pltpu.VMEM((YDIM, ROWS, D), BF),
            pltpu.VMEM((3, ROWS, D), BF),
            pltpu.VMEM((XDIM, 3, 16, 384), BF),
            pltpu.VMEM((3, 3, 16, 384), BF),
            pltpu.VMEM((GROUP, 16, 384), BF),
            pltpu.VMEM((3, 16, 384), BF),
            pltpu.VMEM((16, 384), BF),
            pltpu.VMEM((3, 16, 384), BF),
            pltpu.VMEM((GROUP, 16, 384), BF),
            pltpu.VMEM((XDIM, 3, 16, 384), BF),
            pltpu.VMEM((SPAN, D), BF),
            pltpu.VMEM((SPAN, D), BF),
            pltpu.VMEM((SPAN, D), BF),
            pltpu.VMEM((SPAN, D), BF),
            pltpu.VMEM((D, D), BF),
            pltpu.VMEM((SPAN, D), BF),
            pltpu.VMEM((SPAN, D), BF),
            pltpu.VMEM((SPAN, D), BF),
            pltpu.VMEM((SPAN, D), BF),
            pltpu.VMEM((ROWS, D), F32),
            pltpu.SemaphoreType.DMA((5,)),
            pltpu.SemaphoreType.DMA((5,)),
            pltpu.SemaphoreType.DMA((copies,)),
            pltpu.SemaphoreType.DMA((copies,)),
        ],
        compiler_params=pltpu.CompilerParams(
            collective_id=0, has_side_effects=True, vmem_limit_bytes=67043328
        ),
    )(partner_ids, partner_count, *flat, out_weight)
    return tuple(a.reshape(shape) for a in outs[:4]) + (outs[4],)


def solution(mesh):
    tokens = P("dp", "station", None, None)
    return jax.shard_map(
        local,
        mesh=mesh,
        in_specs=(tokens,) * 4 + (P(), P(), P()),
        out_specs=(tokens,) * 4 + (P("dp", None),),
        check_vma=False,
    )
```

```python
import math

import jax
import jax.numpy as jnp
from jax import lax
from jax.experimental import pallas as pl
from jax.experimental.pallas import tpu as pltpu
from jax.sharding import PartitionSpec as P

HEADS = 12
PMAX = 6
HOPS = 3
SPAN = 128
D = 768
PAIRS = HEADS // 2
STATIONS = 64
ZDIM = 16
XDIM = 4
YDIM = 4
GROUP = 4
DP = 8
ROWS = D // DP
MESH = pl.DeviceIdType.MESH
BF = jnp.bfloat16
F32 = jnp.float32
dead_bias = -1e30
KEY, VALUE, GRAD, QUERY = 0, 1, 2, 3


def dot(a, b, ca=1, cb=0):
    return lax.dot_general(a, b, (((ca,), (cb,)), ((), ())), preferred_element_type=F32)


def kernel(
    ids, cnt, q_in, k_in, v_in, g_in, w_in,
    lo_ref, dq_ref, dk_ref, dv_ref, gw_ref,
    gat, kt, vt, s_buf, bdq, bdm, mixed_t, dq_t, stat, acc_k, acc_v,
    gwp, w1r, ys_a, yr_a, xs_b, xr_b, xs_a, xr_a, ys_b, yr_b, z1s, z1r, z2s, z2r, fin, xfin,
    q_ref, k_ref, v_ref, g_ref, w_ref,
    load, send, recv,
):
    loads = [
        pltpu.make_async_copy(src, dst, load.at[n])
        for n, (src, dst) in enumerate(
            ((w_in, w_ref), (g_in, g_ref), (q_in, q_ref), (k_in, k_ref), (v_in, v_ref))
        )
    ]
    for copy in loads:
        copy.start()
    dp = lax.axis_index("dp")
    me = lax.axis_index("station")
    y, core = dp // 2, dp % 2
    x, z = me // ZDIM, me % ZDIM
    za, zb = z // GROUP, z % GROUP

    def station(offset):
        return (dp, lax.rem(me + offset + STATIONS, STATIONS))

    core_peer = (y * 2 + (1 - core), me)
    y_peers = [(lax.rem(y + o, YDIM) * 2 + core, me) for o in (1, 2, 3)]
    x_peers = [(dp, lax.rem(x + o, XDIM) * ZDIM + z) for o in (1, 2, 3)]
    zb_peers = [(dp, x * ZDIM + za * GROUP + lax.rem(zb + o, GROUP)) for o in (1, 2, 3)]
    za_peers = [(dp, x * ZDIM + lax.rem(za + o, GROUP) * GROUP + zb) for o in (1, 2, 3)]
    near = [station(o) for o in (1, 2, 3, -1, -2, -3)]
    greet = [core_peer] + y_peers + x_peers + zb_peers + za_peers + near
    barrier = pltpu.get_barrier_semaphore()
    for peer in greet:
        pl.semaphore_signal(barrier, inc=1, device_id=peer, device_id_type=MESH)
    pl.semaphore_wait(barrier, len(greet))

    started = []

    def remote(src, dst, number, peer):
        copy = pltpu.make_async_remote_copy(
            src_ref=src, dst_ref=dst, send_sem=send.at[number], recv_sem=recv.at[number],
            device_id=peer, device_id_type=MESH,
        )
        copy.start()
        started.append(copy)
        return copy

    source = (k_in, v_in, g_in, q_in)
    own = (k_ref, v_ref, g_ref, q_ref)
    flights = {}

    def spread(parts, landing, own_index, peers, number):
        count = len(peers) + 1
        return [
            remote(
                parts.at[lax.rem(own_index + o, count)], landing.at[o - 1],
                number + o - 1, peers[o - 1],
            )
            for o in (1, 2, 3)
        ]

    def gathered(copies, parts, landing, own_index):
        for copy in copies:
            copy.wait_recv()
        total = parts[own_index].astype(F32)
        for n in range(3):
            total = total + landing[n].astype(F32)
        return total

    def hop(item, h):
        for way in (0, 1):
            src = source[item] if h == 1 else gat.at[item, way, h - 2]
            flights[item, way, h] = remote(
                src, gat.at[item, way, h - 1], (item * 2 + way) * 3 + h - 1,
                station(1 if way == 0 else -1),
            )

    def arrived(item, h):
        for way in (0, 1):
            flights[item, way, h].wait_recv()

    def block(item, j):
        if j == 0:
            return own[item]
        return gat.at[item, (j - 1) // 3, (j - 1) % 3]

    hop(KEY, 1)
    hop(VALUE, 1)

    offsets = (0, -1, -2, -3, 1, 2, 3)

    def listed(reader, block_station):
        hit = jnp.int32(0)
        for p in range(PMAX):
            same = ids[reader, p] == block_station
            live = p < cnt[reader]
            hit = hit + jnp.where(same & live, jnp.int32(1), jnp.int32(0))
        return jnp.where(hit > 0, F32(0.0), F32(dead_bias))

    bias_f, bias_b = [F32(0.0)], [F32(0.0)]
    for o in offsets[1:]:
        other = station(o)[1]
        bias_f.append(listed(me, other))
        bias_b.append(listed(other, me))

    bdq[...] = jnp.zeros_like(bdq)
    bdm[...] = jnp.zeros_like(bdm)
    for copy in loads:
        copy.wait()

    def prepare(j, slot):
        q_t = block(QUERY, j)[...].T
        q_t = (q_t.astype(F32) * 0.125).astype(BF)
        m_t = dot(w_ref[...], block(GRAD, j)[...], 1, 1).astype(BF)
        for p in range(PAIRS):
            a, b = p * 128, p * 128 + 64
            bdq[slot, p, 0:64, 0:128] = q_t[a : a + 64]
            bdq[slot, p, 64:128, 128:256] = q_t[b : b + 64]
            bdm[slot, p, 0:64, 0:128] = m_t[a : a + 64]
            bdm[slot, p, 64:128, 128:256] = m_t[b : b + 64]

    def turn(j):
        kt[j] = block(KEY, j)[...].T
        vt[j] = block(VALUE, j)[...].T

    prepare(0, 0)
    turn(0)
    for h in (1, 2):
        for item in (KEY, VALUE):
            arrived(item, h)
            hop(item, h + 1)
        if h == 2:
            hop(GRAD, 1)
            hop(QUERY, 1)
        turn(h)
        turn(3 + h)
    arrived(KEY, 3)
    arrived(VALUE, 3)
    turn(3)
    turn(6)

    def forward(p, carry):
        cols = pl.ds(pl.multiple_of(p * 128, 128), 128)
        rhs_q, rhs_m = bdq[0, p], bdm[0, p]
        top = None
        for j in range(7):
            s = dot(block(KEY, j)[:, cols], rhs_q) + bias_f[j]
            s_buf[j] = s
            m = jnp.max(s, 0, keepdims=True)
            top = m if top is None else jnp.maximum(top, m)
        total = jnp.zeros_like(top)
        for j in range(7):
            e = jnp.exp(s_buf[j] - top)
            s_buf[j] = e
            total = total + jnp.sum(e, 0, keepdims=True)
        inv = 1.0 / total
        out = jnp.zeros((128, 256), F32)
        for j in range(7):
            prob = s_buf[j] * inv
            s_buf[j] = prob
            out = out + dot(vt[j, cols, :], prob.astype(BF))
        out = out.astype(BF)
        mixed_t[pl.ds(pl.multiple_of(p * 128, 128), 64), :] = out[0:64, 0:128]
        mixed_t[pl.ds(pl.multiple_of(p * 128 + 64, 64), 64), :] = out[64:128, 128:256]
        delta = jnp.sum(rhs_m.astype(F32) * out.astype(F32), 0, keepdims=True)
        stat[0, pl.ds(p, 1), :] = top + jnp.log(total)
        stat[0, pl.ds(p + 8, 1), :] = delta
        grad = jnp.zeros((128, 256), F32)
        for j in range(7):
            d_prob = dot(block(VALUE, j)[:, cols], rhs_m)
            d_score = (s_buf[j] * (d_prob - delta)).astype(BF)
            grad = grad + dot(kt[j, cols, :], d_score)
        grad = (grad * 0.125).astype(BF)
        dq_t[pl.ds(pl.multiple_of(p * 128, 128), 64), :] = grad[0:64, 0:128]
        dq_t[pl.ds(pl.multiple_of(p * 128 + 64, 64), 64), :] = grad[64:128, 128:256]
        return carry

    lax.fori_loop(0, 4, forward, 0)
    arrived(GRAD, 1)
    hop(GRAD, 2)
    lax.fori_loop(4, PAIRS, forward, 0)

    for d in range(DP):
        rows = mixed_t[d * ROWS : (d + 1) * ROWS, :]
        gwp[d % 2, d // 2] = dot(rows, g_ref[...]).astype(BF)
    core_copy = remote(gwp.at[1 - core], w1r, 30, core_peer)
    stats = []
    for d in (1, 2, 3):
        stats.append(remote(stat.at[0], stat.at[d], 24 + d - 1, station(d)))
        stats.append(remote(stat.at[0], stat.at[3 + d], 27 + d - 1, station(-d)))
    arrived(QUERY, 1)
    hop(QUERY, 2)
    lo_ref[...] = dot(mixed_t[...].T, w_ref[...]).astype(BF)

    core_copy.wait_recv()
    sums = [gwp[core, n].astype(F32) + w1r[n].astype(F32) for n in range(YDIM)]
    for n in range(YDIM):
        ys_a[n] = sums[n][:, 0:384].astype(BF)
    for n in range(XDIM):
        xs_b[n] = jnp.concatenate(
            [sums[m][n * 24 : n * 24 + 24, 384:768] for m in range(YDIM)], 0
        ).astype(BF)
    first_a = spread(ys_a, yr_a, y, y_peers, 31)
    first_b = spread(xs_b, xr_b, x, x_peers, 34)

    dq_ref[...] = dq_t[...].T
    acc_k[...] = jnp.zeros_like(acc_k)
    acc_v[...] = jnp.zeros_like(acc_v)

    def backward(j, slot):
        def step(p, carry):
            cols = pl.ds(pl.multiple_of(p * 128, 128), 128)
            rhs_q, rhs_m = bdq[slot, p], bdm[slot, p]
            shift = bias_b[j] - stat[j, pl.ds(p, 1), :]
            prob = jnp.exp(dot(k_ref[:, cols], rhs_q) + shift)
            d_prob = dot(v_ref[:, cols], rhs_m)
            d_score = (prob * (d_prob - stat[j, pl.ds(p + 8, 1), :])).astype(BF)
            acc_v[:, cols] += dot(prob.astype(BF), rhs_m, 1, 1)
            acc_k[:, cols] += dot(d_score, rhs_q, 1, 1)
            return carry

        lax.fori_loop(0, PAIRS, step, 0)

    backward(0, 0)
    arrived(GRAD, 2)
    hop(GRAD, 3)
    for copy in stats:
        copy.wait_recv()
    prepare(1, 1)
    backward(1, 1)
    arrived(QUERY, 2)
    hop(QUERY, 3)
    total = gathered(first_a, ys_a, yr_a, y)
    for n in range(XDIM):
        xs_a[n] = total[n * 24 : n * 24 + 24].astype(BF)
    second_a = spread(xs_a, xr_a, x, x_peers, 49)
    total = gathered(first_b, xs_b, xr_b, x)
    for n in range(YDIM):
        ys_b[n] = total[n * 24 : n * 24 + 24].astype(BF)
    second_b = spread(ys_b, yr_b, y, y_peers, 52)
    prepare(4, 0)
    backward(4, 0)

    half_a = gathered(second_a, xs_a, xr_a, x)
    half_b = gathered(second_b, ys_b, yr_b, y)
    for r in range(3):
        z1s[r] = jnp.concatenate(
            [half_a[r * 8 : r * 8 + 8], half_b[r * 8 : r * 8 + 8]], 0
        ).astype(BF)
    z1s[3] = jnp.zeros_like(z1s[3])
    zb_copies = [
        remote(z1s.at[lax.rem(zb + o, GROUP)], z1r.at[o - 1], 37 + o - 1, zb_peers[o - 1])
        for o in (1, 2, 3)
    ]
    prepare(2, 1)
    backward(2, 1)

    for copy in zb_copies:
        copy.wait_recv()
    part = z1s[zb].astype(F32)
    for n in range(3):
        part = part + z1r[n].astype(F32)
    z2s[...] = part.astype(BF)
    za_copies = [remote(z2s, z2r.at[o - 1], 40 + o - 1, za_peers[o - 1]) for o in (1, 2, 3)]

    prepare(5, 0)
    backward(5, 0)
    arrived(GRAD, 3)
    arrived(QUERY, 3)
    prepare(3, 1)
    backward(3, 1)
    prepare(6, 0)
    backward(6, 0)
    dk_ref[...] = acc_k[...].astype(BF)
    dv_ref[...] = acc_v[...].astype(BF)

    for copy in za_copies:
        copy.wait_recv()
    part = z2s[...].astype(F32)
    for n in range(3):
        part = part + z2r[n].astype(F32)
    fin[zb] = (part * (1.0 / math.sqrt(DP * STATIONS * SPAN))).astype(BF)
    zb_copies = [remote(fin.at[zb], fin.at[zb], 43 + o - 1, zb_peers[o - 1]) for o in (1, 2, 3)]
    for copy in zb_copies:
        copy.wait_recv()
    x_copies = [
        remote(fin.at[pl.ds(0, 3)], xfin.at[x], 46 + o - 1, x_peers[o - 1]) for o in (1, 2, 3)
    ]
    xfin[x] = fin[0:3]
    for copy in x_copies:
        copy.wait_recv()
    for n in range(XDIM):
        for r in range(3):
            lower = n * 24 + r * 8
            piece = xfin[n, r].astype(F32)
            gw_ref[lower : lower + 8, 0:384] = piece[0:8]
            gw_ref[lower : lower + 8, 384:768] = piece[8:16]
    for copy in started:
        copy.wait_send()


def local(
    query_states, key_states, value_states, grad_output, out_weight, partner_ids, partner_count
):
    shape = query_states.shape
    flat = [
        pltpu.with_memory_space_constraint(a.reshape(SPAN, D), pltpu.HBM)
        for a in (query_states, key_states, value_states, grad_output)
    ]
    out_weight = pltpu.with_memory_space_constraint(out_weight, pltpu.HBM)
    hbm = pl.BlockSpec(memory_space=pltpu.HBM)
    vmem = pl.BlockSpec(memory_space=pltpu.VMEM)
    smem = pl.BlockSpec(memory_space=pltpu.SMEM)
    rows = jax.ShapeDtypeStruct((SPAN, D), BF)
    copies = 55
    outs = pl.pallas_call(
        kernel,
        out_shape=(rows, rows, rows, rows, jax.ShapeDtypeStruct((ROWS, D), F32)),
        in_specs=[smem, smem] + [hbm] * 5,
        out_specs=(vmem,) * 5,
        scratch_shapes=[
            pltpu.VMEM((4, 2, HOPS, SPAN, D), BF),
            pltpu.VMEM((7, D, SPAN), BF),
            pltpu.VMEM((7, D, SPAN), BF),
            pltpu.VMEM((7, SPAN, 256), F32),
            pltpu.VMEM((2, PAIRS, 128, 256), BF),
            pltpu.VMEM((2, PAIRS, 128, 256), BF),
            pltpu.VMEM((D, SPAN), BF),
            pltpu.VMEM((D, SPAN), BF),
            pltpu.VMEM((7, 16, 256), F32),
            pltpu.VMEM((SPAN, D), F32),
            pltpu.VMEM((SPAN, D), F32),
            pltpu.VMEM((2, YDIM, ROWS, D), BF),
            pltpu.VMEM((YDIM, ROWS, D), BF),
            pltpu.VMEM((YDIM, ROWS, 384), BF),
            pltpu.VMEM((3, ROWS, 384), BF),
            pltpu.VMEM((XDIM, ROWS, 384), BF),
            pltpu.VMEM((3, ROWS, 384), BF),
            pltpu.VMEM((XDIM, 24, 384), BF),
            pltpu.VMEM((3, 24, 384), BF),
            pltpu.VMEM((YDIM, 24, 384), BF),
            pltpu.VMEM((3, 24, 384), BF),
            pltpu.VMEM((GROUP, 16, 384), BF),
            pltpu.VMEM((3, 16, 384), BF),
            pltpu.VMEM((16, 384), BF),
            pltpu.VMEM((3, 16, 384), BF),
            pltpu.VMEM((GROUP, 16, 384), BF),
            pltpu.VMEM((XDIM, 3, 16, 384), BF),
            pltpu.VMEM((SPAN, D), BF),
            pltpu.VMEM((SPAN, D), BF),
            pltpu.VMEM((SPAN, D), BF),
            pltpu.VMEM((SPAN, D), BF),
            pltpu.VMEM((D, D), BF),
            pltpu.SemaphoreType.DMA((5,)),
            pltpu.SemaphoreType.DMA((copies,)),
            pltpu.SemaphoreType.DMA((copies,)),
        ],
        compiler_params=pltpu.CompilerParams(
            collective_id=0, has_side_effects=True, vmem_limit_bytes=40 * 1024 * 1024
        ),
    )(partner_ids, partner_count, *flat, out_weight)
    return tuple(a.reshape(shape) for a in outs[:4]) + (outs[4],)


def solution(mesh):
    tokens = P("dp", "station", None, None)
    return jax.shard_map(
        local,
        mesh=mesh,
        in_specs=(tokens,) * 4 + (P(), P(), P()),
        out_specs=(tokens,) * 4 + (P("dp", None),),
        check_vma=False,
    )
```

```python
import math

import jax
import jax.numpy as jnp
from jax import lax
from jax.experimental import pallas as pl
from jax.experimental.pallas import tpu as pltpu
from jax.sharding import PartitionSpec as P

HEADS = 12
PMAX = 6
HOPS = 3
SPAN = 128
D = 768
PAIRS = HEADS // 2
STATIONS = 64
ZDIM = 16
XDIM = 4
YDIM = 4
GROUP = 4
DP = 8
ROWS = D // DP
MESH = pl.DeviceIdType.MESH
BF = jnp.bfloat16
F32 = jnp.float32
dead_bias = -1e30
KEY, VALUE, GRAD, QUERY = 0, 1, 2, 3


def dot(a, b, ca=1, cb=0):
    return lax.dot_general(a, b, (((ca,), (cb,)), ((), ())), preferred_element_type=F32)


def kernel(
    ids, cnt, q_in, k_in, v_in, g_in, w_in,
    lo_ref, dq_ref, dk_ref, dv_ref, gw_ref,
    gat, kt, vt, s_buf, bdq, bdm, mixed_t, dq_t, stat, acc_k, acc_v,
    gwp, w1r, ys, yr, ps, pr, z2s, z2r, fin, xfin,
    q_ref, k_ref, v_ref, g_ref, w_ref,
    load, send, recv,
):
    loads = [
        pltpu.make_async_copy(src, dst, load.at[n])
        for n, (src, dst) in enumerate(
            ((w_in, w_ref), (g_in, g_ref), (q_in, q_ref), (k_in, k_ref), (v_in, v_ref))
        )
    ]
    for copy in loads:
        copy.start()
    dp = lax.axis_index("dp")
    me = lax.axis_index("station")
    y, core = dp // 2, dp % 2
    x, z = me // ZDIM, me % ZDIM
    za, zb = z // GROUP, z % GROUP

    def station(offset):
        return (dp, lax.rem(me + offset + STATIONS, STATIONS))

    core_peer = (y * 2 + (1 - core), me)
    y_peers = [(lax.rem(y + o, YDIM) * 2 + core, me) for o in (1, 2, 3)]
    block_peers = [
        (dp, lax.rem(x + o // GROUP, XDIM) * ZDIM + za * GROUP + lax.rem(zb + o % GROUP, GROUP))
        for o in range(1, XDIM * GROUP)
    ]
    za_peers = [(dp, x * ZDIM + lax.rem(za + o, GROUP) * GROUP + zb) for o in (1, 2, 3)]
    near = [station(o) for o in (1, 2, 3, -1, -2, -3)]
    greet = [core_peer] + y_peers + block_peers + za_peers + near
    barrier = pltpu.get_barrier_semaphore()
    for peer in greet:
        pl.semaphore_signal(barrier, inc=1, device_id=peer, device_id_type=MESH)
    pl.semaphore_wait(barrier, len(greet))

    started = []

    def remote(src, dst, number, peer):
        copy = pltpu.make_async_remote_copy(
            src_ref=src, dst_ref=dst, send_sem=send.at[number], recv_sem=recv.at[number],
            device_id=peer, device_id_type=MESH,
        )
        copy.start()
        started.append(copy)
        return copy

    source = (k_in, v_in, g_in, q_in)
    own = (k_ref, v_ref, g_ref, q_ref)
    flights = {}

    def hop(item, h):
        for way in (0, 1):
            src = source[item] if h == 1 else gat.at[item, way, h - 2]
            flights[item, way, h] = remote(
                src, gat.at[item, way, h - 1], (item * 2 + way) * 3 + h - 1,
                station(1 if way == 0 else -1),
            )

    def arrived(item, h):
        for way in (0, 1):
            flights[item, way, h].wait_recv()

    def block(item, j):
        if j == 0:
            return own[item]
        return gat.at[item, (j - 1) // 3, (j - 1) % 3]

    hop(KEY, 1)
    hop(VALUE, 1)

    offsets = (0, -1, -2, -3, 1, 2, 3)

    def listed(reader, block_station):
        hit = jnp.int32(0)
        for p in range(PMAX):
            same = ids[reader, p] == block_station
            live = p < cnt[reader]
            hit = hit + jnp.where(same & live, jnp.int32(1), jnp.int32(0))
        return jnp.where(hit > 0, F32(0.0), F32(dead_bias))

    bias_f, bias_b = [F32(0.0)], [F32(0.0)]
    for o in offsets[1:]:
        other = station(o)[1]
        bias_f.append(listed(me, other))
        bias_b.append(listed(other, me))

    bdq[...] = jnp.zeros_like(bdq)
    bdm[...] = jnp.zeros_like(bdm)
    for copy in loads:
        copy.wait()

    def prepare(j, slot):
        q_t = block(QUERY, j)[...].T
        q_t = (q_t.astype(F32) * 0.125).astype(BF)
        m_t = dot(w_ref[...], block(GRAD, j)[...], 1, 1).astype(BF)
        for p in range(PAIRS):
            a, b = p * 128, p * 128 + 64
            bdq[slot, p, 0:64, 0:128] = q_t[a : a + 64]
            bdq[slot, p, 64:128, 128:256] = q_t[b : b + 64]
            bdm[slot, p, 0:64, 0:128] = m_t[a : a + 64]
            bdm[slot, p, 64:128, 128:256] = m_t[b : b + 64]

    def turn(j):
        kt[j] = block(KEY, j)[...].T
        vt[j] = block(VALUE, j)[...].T

    prepare(0, 0)
    turn(0)
    for h in (1, 2):
        for item in (KEY, VALUE):
            arrived(item, h)
            hop(item, h + 1)
        if h == 2:
            hop(GRAD, 1)
            hop(QUERY, 1)
        turn(h)
        turn(3 + h)
    arrived(KEY, 3)
    arrived(VALUE, 3)
    turn(3)
    turn(6)

    def forward(p, carry):
        cols = pl.ds(pl.multiple_of(p * 128, 128), 128)
        rhs_q, rhs_m = bdq[0, p], bdm[0, p]
        top = None
        for j in range(7):
            s = dot(block(KEY, j)[:, cols], rhs_q) + bias_f[j]
            s_buf[j] = s
            m = jnp.max(s, 0, keepdims=True)
            top = m if top is None else jnp.maximum(top, m)
        total = jnp.zeros_like(top)
        for j in range(7):
            e = jnp.exp(s_buf[j] - top)
            s_buf[j] = e
            total = total + jnp.sum(e, 0, keepdims=True)
        inv = 1.0 / total
        out = jnp.zeros((128, 256), F32)
        for j in range(7):
            prob = s_buf[j] * inv
            s_buf[j] = prob
            out = out + dot(vt[j, cols, :], prob.astype(BF))
        out = out.astype(BF)
        mixed_t[pl.ds(pl.multiple_of(p * 128, 128), 64), :] = out[0:64, 0:128]
        mixed_t[pl.ds(pl.multiple_of(p * 128 + 64, 64), 64), :] = out[64:128, 128:256]
        delta = jnp.sum(rhs_m.astype(F32) * out.astype(F32), 0, keepdims=True)
        stat[0, pl.ds(p, 1), :] = top + jnp.log(total)
        stat[0, pl.ds(p + 8, 1), :] = delta
        grad = jnp.zeros((128, 256), F32)
        for j in range(7):
            d_prob = dot(block(VALUE, j)[:, cols], rhs_m)
            d_score = (s_buf[j] * (d_prob - delta)).astype(BF)
            grad = grad + dot(kt[j, cols, :], d_score)
        grad = (grad * 0.125).astype(BF)
        dq_t[pl.ds(pl.multiple_of(p * 128, 128), 64), :] = grad[0:64, 0:128]
        dq_t[pl.ds(pl.multiple_of(p * 128 + 64, 64), 64), :] = grad[64:128, 128:256]
        return carry

    lax.fori_loop(0, 4, forward, 0)
    arrived(GRAD, 1)
    hop(GRAD, 2)
    lax.fori_loop(4, PAIRS, forward, 0)

    for d in range(DP):
        rows = mixed_t[d * ROWS : (d + 1) * ROWS, :]
        gwp[d % 2, d // 2] = dot(rows, g_ref[...]).astype(BF)
    core_copy = remote(gwp.at[1 - core], w1r, 30, core_peer)
    stats = []
    for d in (1, 2, 3):
        stats.append(remote(stat.at[0], stat.at[d], 24 + d - 1, station(d)))
        stats.append(remote(stat.at[0], stat.at[3 + d], 27 + d - 1, station(-d)))
    arrived(QUERY, 1)
    hop(QUERY, 2)
    lo_ref[...] = dot(mixed_t[...].T, w_ref[...]).astype(BF)

    core_copy.wait_recv()
    for n in range(YDIM):
        ys[n] = (gwp[core, n].astype(F32) + w1r[n].astype(F32)).astype(BF)
    y_copies = [
        remote(ys.at[lax.rem(y + o, YDIM)], yr.at[o - 1], 31 + o - 1, y_peers[o - 1])
        for o in (1, 2, 3)
    ]

    dq_ref[...] = dq_t[...].T
    acc_k[...] = jnp.zeros_like(acc_k)
    acc_v[...] = jnp.zeros_like(acc_v)

    def backward(j, slot):
        def step(p, carry):
            cols = pl.ds(pl.multiple_of(p * 128, 128), 128)
            rhs_q, rhs_m = bdq[slot, p], bdm[slot, p]
            shift = bias_b[j] - stat[j, pl.ds(p, 1), :]
            prob = jnp.exp(dot(k_ref[:, cols], rhs_q) + shift)
            d_prob = dot(v_ref[:, cols], rhs_m)
            d_score = (prob * (d_prob - stat[j, pl.ds(p + 8, 1), :])).astype(BF)
            acc_v[:, cols] += dot(prob.astype(BF), rhs_m, 1, 1)
            acc_k[:, cols] += dot(d_score, rhs_q, 1, 1)
            return carry

        lax.fori_loop(0, PAIRS, step, 0)

    backward(0, 0)
    arrived(GRAD, 2)
    hop(GRAD, 3)
    for copy in stats:
        copy.wait_recv()
    prepare(1, 1)
    backward(1, 1)
    arrived(QUERY, 2)
    hop(QUERY, 3)
    prepare(4, 0)
    backward(4, 0)

    for copy in y_copies:
        copy.wait_recv()
    total = ys[y].astype(F32)
    for n in range(3):
        total = total + yr[n].astype(F32)
    for n in range(XDIM):
        for r in range(3):
            lower = n * 24 + r * 8
            piece = total[lower : lower + 8]
            ps[n, r] = jnp.concatenate([piece[:, 0:384], piece[:, 384:768]], 0).astype(BF)
        ps[n, 3] = jnp.zeros((16, 384), BF)
    block_copies = [
        remote(
            ps.at[lax.rem(x + o // GROUP, XDIM), lax.rem(zb + o % GROUP, GROUP)],
            pr.at[o - 1], 34 + o - 1, block_peers[o - 1],
        )
        for o in range(1, XDIM * GROUP)
    ]
    prepare(2, 1)
    backward(2, 1)

    for copy in block_copies:
        copy.wait_recv()
    part = ps[x, zb].astype(F32)
    for n in range(XDIM * GROUP - 1):
        part = part + pr[n].astype(F32)
    z2s[...] = part.astype(BF)
    za_copies = [remote(z2s, z2r.at[o - 1], 64 + o - 1, za_peers[o - 1]) for o in (1, 2, 3)]

    prepare(5, 0)
    backward(5, 0)
    arrived(GRAD, 3)
    arrived(QUERY, 3)
    prepare(3, 1)
    backward(3, 1)
    prepare(6, 0)
    backward(6, 0)
    dk_ref[...] = acc_k[...].astype(BF)
    dv_ref[...] = acc_v[...].astype(BF)

    for copy in za_copies:
        copy.wait_recv()
    part = z2s[...].astype(F32)
    for n in range(3):
        part = part + z2r[n].astype(F32)
    fin[...] = (part * (1.0 / math.sqrt(DP * STATIONS * SPAN))).astype(BF)
    block_copies = [
        remote(fin, xfin.at[x, zb], 49 + o - 1, block_peers[o - 1])
        for o in range(1, XDIM * GROUP)
    ]
    xfin[x, zb] = fin[...]
    for copy in block_copies:
        copy.wait_recv()
    for n in range(XDIM):
        for r in range(3):
            lower = n * 24 + r * 8
            piece = xfin[n, r].astype(F32)
            gw_ref[lower : lower + 8, 0:384] = piece[0:8]
            gw_ref[lower : lower + 8, 384:768] = piece[8:16]
    for copy in started:
        copy.wait_send()


def local(
    query_states, key_states, value_states, grad_output, out_weight, partner_ids, partner_count
):
    shape = query_states.shape
    flat = [
        pltpu.with_memory_space_constraint(a.reshape(SPAN, D), pltpu.HBM)
        for a in (query_states, key_states, value_states, grad_output)
    ]
    out_weight = pltpu.with_memory_space_constraint(out_weight, pltpu.HBM)
    hbm = pl.BlockSpec(memory_space=pltpu.HBM)
    vmem = pl.BlockSpec(memory_space=pltpu.VMEM)
    smem = pl.BlockSpec(memory_space=pltpu.SMEM)
    rows = jax.ShapeDtypeStruct((SPAN, D), BF)
    copies = 67
    outs = pl.pallas_call(
        kernel,
        out_shape=(rows, rows, rows, rows, jax.ShapeDtypeStruct((ROWS, D), F32)),
        in_specs=[smem, smem] + [hbm] * 5,
        out_specs=(vmem,) * 5,
        scratch_shapes=[
            pltpu.VMEM((4, 2, HOPS, SPAN, D), BF),
            pltpu.VMEM((7, D, SPAN), BF),
            pltpu.VMEM((7, D, SPAN), BF),
            pltpu.VMEM((7, SPAN, 256), F32),
            pltpu.VMEM((2, PAIRS, 128, 256), BF),
            pltpu.VMEM((2, PAIRS, 128, 256), BF),
            pltpu.VMEM((D, SPAN), BF),
            pltpu.VMEM((D, SPAN), BF),
            pltpu.VMEM((7, 16, 256), F32),
            pltpu.VMEM((SPAN, D), F32),
            pltpu.VMEM((SPAN, D), F32),
            pltpu.VMEM((2, YDIM, ROWS, D), BF),
            pltpu.VMEM((YDIM, ROWS, D), BF),
            pltpu.VMEM((YDIM, ROWS, D), BF),
            pltpu.VMEM((3, ROWS, D), BF),
            pltpu.VMEM((XDIM, GROUP, 16, 384), BF),
            pltpu.VMEM((XDIM * GROUP - 1, 16, 384), BF),
            pltpu.VMEM((16, 384), BF),
            pltpu.VMEM((3, 16, 384), BF),
            pltpu.VMEM((16, 384), BF),
            pltpu.VMEM((XDIM, GROUP, 16, 384), BF),
            pltpu.VMEM((SPAN, D), BF),
            pltpu.VMEM((SPAN, D), BF),
            pltpu.VMEM((SPAN, D), BF),
            pltpu.VMEM((SPAN, D), BF),
            pltpu.VMEM((D, D), BF),
            pltpu.SemaphoreType.DMA((5,)),
            pltpu.SemaphoreType.DMA((copies,)),
            pltpu.SemaphoreType.DMA((copies,)),
        ],
        compiler_params=pltpu.CompilerParams(
            collective_id=0, has_side_effects=True, vmem_limit_bytes=40 * 1024 * 1024
        ),
    )(partner_ids, partner_count, *flat, out_weight)
    return tuple(a.reshape(shape) for a in outs[:4]) + (outs[4],)


def solution(mesh):
    tokens = P("dp", "station", None, None)
    return jax.shard_map(
        local,
        mesh=mesh,
        in_specs=(tokens,) * 4 + (P(), P(), P()),
        out_specs=(tokens,) * 4 + (P("dp", None),),
        check_vma=False,
    )
```

```python
import math

import jax
import jax.numpy as jnp
from jax import lax
from jax.experimental import pallas as pl
from jax.experimental.pallas import tpu as pltpu
from jax.sharding import PartitionSpec as P

HEADS = 12
PMAX = 6
HOPS = 3
SPAN = 128
D = 768
PAIRS = HEADS // 2
STATIONS = 64
ZDIM = 16
XDIM = 4
YDIM = 4
GROUP = 4
DP = 8
ROWS = D // DP
MESH = pl.DeviceIdType.MESH
BF = jnp.bfloat16
F32 = jnp.float32
dead_bias = -1e30
KEY, VALUE, GRAD, QUERY = 0, 1, 2, 3


def dot(a, b, ca=1, cb=0):
    return lax.dot_general(a, b, (((ca,), (cb,)), ((), ())), preferred_element_type=F32)


def kernel(
    ids, cnt, q_in, k_in, v_in, g_in, w_in,
    lo_ref, dq_ref, dk_ref, dv_ref, gw_ref,
    gat, kt, vt, s_buf, out_buf, bdq, bdm, mixed_t, dq_t, stat, acc_k, acc_v,
    gwp, w1r, ys, yr, ps, pr, z2s, z2r, fin, xfin,
    q_ref, k_ref, v_ref, g_ref, w_ref,
    load, send, recv,
):
    loads = [
        pltpu.make_async_copy(src, dst, load.at[n])
        for n, (src, dst) in enumerate(
            ((w_in, w_ref), (g_in, g_ref), (q_in, q_ref), (k_in, k_ref), (v_in, v_ref))
        )
    ]
    for copy in loads:
        copy.start()
    dp = lax.axis_index("dp")
    me = lax.axis_index("station")
    y, core = dp // 2, dp % 2
    x, z = me // ZDIM, me % ZDIM
    za, zb = z // GROUP, z % GROUP

    def station(offset):
        return (dp, lax.rem(me + offset + STATIONS, STATIONS))

    core_peer = (y * 2 + (1 - core), me)
    y_peers = [(lax.rem(y + o, YDIM) * 2 + core, me) for o in (1, 2, 3)]
    block_peers = [
        (dp, lax.rem(x + o // GROUP, XDIM) * ZDIM + za * GROUP + lax.rem(zb + o % GROUP, GROUP))
        for o in range(1, XDIM * GROUP)
    ]
    za_peers = [(dp, x * ZDIM + lax.rem(za + o, GROUP) * GROUP + zb) for o in (1, 2, 3)]
    near = [station(o) for o in (1, 2, 3, -1, -2, -3)]
    greet = [core_peer] + y_peers + block_peers + za_peers + near
    barrier = pltpu.get_barrier_semaphore()
    for peer in greet:
        pl.semaphore_signal(barrier, inc=1, device_id=peer, device_id_type=MESH)
    pl.semaphore_wait(barrier, len(greet))

    started = []

    def remote(src, dst, number, peer):
        copy = pltpu.make_async_remote_copy(
            src_ref=src, dst_ref=dst, send_sem=send.at[number], recv_sem=recv.at[number],
            device_id=peer, device_id_type=MESH,
        )
        copy.start()
        started.append(copy)
        return copy

    source = (k_in, v_in, g_in, q_in)
    own = (k_ref, v_ref, g_ref, q_ref)
    flights = {}

    def hop(item, h):
        for way in (0, 1):
            src = source[item] if h == 1 else gat.at[item, way, h - 2]
            flights[item, way, h] = remote(
                src, gat.at[item, way, h - 1], (item * 2 + way) * 3 + h - 1,
                station(1 if way == 0 else -1),
            )

    def arrived(item, h):
        for way in (0, 1):
            flights[item, way, h].wait_recv()

    def block(item, j):
        if j == 0:
            return own[item]
        return gat.at[item, (j - 1) // 3, (j - 1) % 3]

    hop(KEY, 1)
    hop(VALUE, 1)

    offsets = (0, -1, -2, -3, 1, 2, 3)

    def listed(reader, block_station):
        hit = jnp.int32(0)
        for p in range(PMAX):
            same = ids[reader, p] == block_station
            live = p < cnt[reader]
            hit = hit + jnp.where(same & live, jnp.int32(1), jnp.int32(0))
        return jnp.where(hit > 0, F32(0.0), F32(dead_bias))

    bias_f, bias_b = [F32(0.0)], [F32(0.0)]
    for o in offsets[1:]:
        other = station(o)[1]
        bias_f.append(listed(me, other))
        bias_b.append(listed(other, me))

    bdq[...] = jnp.zeros_like(bdq)
    bdm[...] = jnp.zeros_like(bdm)
    for copy in loads:
        copy.wait()

    def prepare(j, slot):
        q_t = block(QUERY, j)[...].T
        q_t = (q_t.astype(F32) * 0.125).astype(BF)
        m_t = dot(w_ref[...], block(GRAD, j)[...], 1, 1).astype(BF)
        for p in range(PAIRS):
            a, b = p * 128, p * 128 + 64
            bdq[slot, p, 0:64, 0:128] = q_t[a : a + 64]
            bdq[slot, p, 64:128, 128:256] = q_t[b : b + 64]
            bdm[slot, p, 0:64, 0:128] = m_t[a : a + 64]
            bdm[slot, p, 64:128, 128:256] = m_t[b : b + 64]

    def flip(item, turned, j):
        turned[j] = block(item, j)[...].T

    def turn(j):
        flip(KEY, kt, j)
        flip(VALUE, vt, j)

    prepare(0, 0)
    turn(0)
    for h in (1, 2):
        for item in (KEY, VALUE):
            arrived(item, h)
            hop(item, h + 1)
        if h == 2:
            hop(GRAD, 1)
            hop(QUERY, 1)
        turn(h)
        turn(3 + h)
    arrived(KEY, 3)
    arrived(VALUE, 3)
    flip(VALUE, vt, 3)
    flip(VALUE, vt, 6)

    def forward(p, carry):
        cols = pl.ds(pl.multiple_of(p * 128, 128), 128)
        rhs_q = bdq[0, p]
        top = None
        for j in range(7):
            s = dot(block(KEY, j)[:, cols], rhs_q) + bias_f[j]
            s_buf[p, j] = s
            m = jnp.max(s, 0, keepdims=True)
            top = m if top is None else jnp.maximum(top, m)
        total = jnp.zeros_like(top)
        for j in range(7):
            e = jnp.exp(s_buf[p, j] - top)
            s_buf[p, j] = e
            total = total + jnp.sum(e, 0, keepdims=True)
        inv = 1.0 / total
        out = jnp.zeros((128, 256), F32)
        for j in range(7):
            prob = s_buf[p, j] * inv
            s_buf[p, j] = prob
            out = out + dot(vt[j, cols, :], prob.astype(BF))
        out = out.astype(BF)
        out_buf[p] = out
        mixed_t[pl.ds(pl.multiple_of(p * 128, 128), 64), :] = out[0:64, 0:128]
        mixed_t[pl.ds(pl.multiple_of(p * 128 + 64, 64), 64), :] = out[64:128, 128:256]
        stat[0, pl.ds(p, 1), :] = top + jnp.log(total)
        return carry

    def query_side(p, carry):
        cols = pl.ds(pl.multiple_of(p * 128, 128), 128)
        rhs_m = bdm[0, p]
        delta = jnp.sum(rhs_m.astype(F32) * out_buf[p].astype(F32), 0, keepdims=True)
        stat[0, pl.ds(p + 8, 1), :] = delta
        grad = jnp.zeros((128, 256), F32)
        for j in range(7):
            d_prob = dot(block(VALUE, j)[:, cols], rhs_m)
            d_score = (s_buf[p, j] * (d_prob - delta)).astype(BF)
            grad = grad + dot(kt[j, cols, :], d_score)
        grad = (grad * 0.125).astype(BF)
        dq_t[pl.ds(pl.multiple_of(p * 128, 128), 64), :] = grad[0:64, 0:128]
        dq_t[pl.ds(pl.multiple_of(p * 128 + 64, 64), 64), :] = grad[64:128, 128:256]
        return carry

    lax.fori_loop(0, 4, forward, 0)
    arrived(GRAD, 1)
    hop(GRAD, 2)
    lax.fori_loop(4, PAIRS, forward, 0)

    for d in range(DP):
        rows = mixed_t[d * ROWS : (d + 1) * ROWS, :]
        gwp[d % 2, d // 2] = dot(rows, g_ref[...]).astype(BF)
    core_copy = remote(gwp.at[1 - core], w1r, 30, core_peer)
    arrived(QUERY, 1)
    hop(QUERY, 2)
    flip(KEY, kt, 3)
    flip(KEY, kt, 6)
    lax.fori_loop(0, PAIRS, query_side, 0)
    stats = []
    for d in (1, 2, 3):
        stats.append(remote(stat.at[0], stat.at[d], 24 + d - 1, station(d)))
        stats.append(remote(stat.at[0], stat.at[3 + d], 27 + d - 1, station(-d)))
    core_copy.wait_recv()
    for n in range(YDIM):
        ys[n] = (gwp[core, n].astype(F32) + w1r[n].astype(F32)).astype(BF)
    y_copies = [
        remote(ys.at[lax.rem(y + o, YDIM)], yr.at[o - 1], 31 + o - 1, y_peers[o - 1])
        for o in (1, 2, 3)
    ]

    lo_ref[...] = dot(mixed_t[...].T, w_ref[...]).astype(BF)
    dq_ref[...] = dq_t[...].T
    acc_k[...] = jnp.zeros_like(acc_k)
    acc_v[...] = jnp.zeros_like(acc_v)

    def backward(j, slot):
        def step(p, carry):
            cols = pl.ds(pl.multiple_of(p * 128, 128), 128)
            rhs_q, rhs_m = bdq[slot, p], bdm[slot, p]
            shift = bias_b[j] - stat[j, pl.ds(p, 1), :]
            prob = jnp.exp(dot(k_ref[:, cols], rhs_q) + shift)
            d_prob = dot(v_ref[:, cols], rhs_m)
            d_score = (prob * (d_prob - stat[j, pl.ds(p + 8, 1), :])).astype(BF)
            acc_v[:, cols] += dot(prob.astype(BF), rhs_m, 1, 1)
            acc_k[:, cols] += dot(d_score, rhs_q, 1, 1)
            return carry

        lax.fori_loop(0, PAIRS, step, 0)

    backward(0, 0)
    arrived(GRAD, 2)
    hop(GRAD, 3)
    for copy in stats:
        copy.wait_recv()
    prepare(1, 1)
    backward(1, 1)
    arrived(QUERY, 2)
    hop(QUERY, 3)
    prepare(4, 0)
    backward(4, 0)
    prepare(2, 1)
    backward(2, 1)

    for copy in y_copies:
        copy.wait_recv()
    total = ys[y].astype(F32)
    for n in range(3):
        total = total + yr[n].astype(F32)
    for n in range(XDIM):
        for r in range(3):
            lower = n * 24 + r * 8
            piece = total[lower : lower + 8]
            ps[n, r] = jnp.concatenate([piece[:, 0:384], piece[:, 384:768]], 0).astype(BF)
        ps[n, 3] = jnp.zeros((16, 384), BF)
    block_copies = [
        remote(
            ps.at[lax.rem(x + o // GROUP, XDIM), lax.rem(zb + o % GROUP, GROUP)],
            pr.at[o - 1], 34 + o - 1, block_peers[o - 1],
        )
        for o in range(1, XDIM * GROUP)
    ]
    prepare(5, 0)
    backward(5, 0)

    for copy in block_copies:
        copy.wait_recv()
    part = ps[x, zb].astype(F32)
    for n in range(XDIM * GROUP - 1):
        part = part + pr[n].astype(F32)
    z2s[...] = part.astype(BF)
    za_copies = [remote(z2s, z2r.at[o - 1], 64 + o - 1, za_peers[o - 1]) for o in (1, 2, 3)]

    arrived(GRAD, 3)
    arrived(QUERY, 3)
    prepare(3, 1)
    backward(3, 1)

    for copy in za_copies:
        copy.wait_recv()
    part = z2s[...].astype(F32)
    for n in range(3):
        part = part + z2r[n].astype(F32)
    fin[...] = (part * (1.0 / math.sqrt(DP * STATIONS * SPAN))).astype(BF)
    block_copies = [
        remote(fin, xfin.at[x, zb], 49 + o - 1, block_peers[o - 1])
        for o in range(1, XDIM * GROUP)
    ]
    xfin[x, zb] = fin[...]
    prepare(6, 0)
    backward(6, 0)
    dk_ref[...] = acc_k[...].astype(BF)
    dv_ref[...] = acc_v[...].astype(BF)
    for copy in block_copies:
        copy.wait_recv()
    for n in range(XDIM):
        for r in range(3):
            lower = n * 24 + r * 8
            piece = xfin[n, r].astype(F32)
            gw_ref[lower : lower + 8, 0:384] = piece[0:8]
            gw_ref[lower : lower + 8, 384:768] = piece[8:16]
    for copy in started:
        copy.wait_send()


def local(
    query_states, key_states, value_states, grad_output, out_weight, partner_ids, partner_count
):
    shape = query_states.shape
    flat = [
        pltpu.with_memory_space_constraint(a.reshape(SPAN, D), pltpu.HBM)
        for a in (query_states, key_states, value_states, grad_output)
    ]
    out_weight = pltpu.with_memory_space_constraint(out_weight, pltpu.HBM)
    hbm = pl.BlockSpec(memory_space=pltpu.HBM)
    vmem = pl.BlockSpec(memory_space=pltpu.VMEM)
    smem = pl.BlockSpec(memory_space=pltpu.SMEM)
    rows = jax.ShapeDtypeStruct((SPAN, D), BF)
    copies = 67
    outs = pl.pallas_call(
        kernel,
        out_shape=(rows, rows, rows, rows, jax.ShapeDtypeStruct((ROWS, D), F32)),
        in_specs=[smem, smem] + [hbm] * 5,
        out_specs=(vmem,) * 5,
        scratch_shapes=[
            pltpu.VMEM((4, 2, HOPS, SPAN, D), BF),
            pltpu.VMEM((7, D, SPAN), BF),
            pltpu.VMEM((7, D, SPAN), BF),
            pltpu.VMEM((PAIRS, 7, SPAN, 256), F32),
            pltpu.VMEM((PAIRS, 128, 256), BF),
            pltpu.VMEM((2, PAIRS, 128, 256), BF),
            pltpu.VMEM((2, PAIRS, 128, 256), BF),
            pltpu.VMEM((D, SPAN), BF),
            pltpu.VMEM((D, SPAN), BF),
            pltpu.VMEM((7, 16, 256), F32),
            pltpu.VMEM((SPAN, D), F32),
            pltpu.VMEM((SPAN, D), F32),
            pltpu.VMEM((2, YDIM, ROWS, D), BF),
            pltpu.VMEM((YDIM, ROWS, D), BF),
            pltpu.VMEM((YDIM, ROWS, D), BF),
            pltpu.VMEM((3, ROWS, D), BF),
            pltpu.VMEM((XDIM, GROUP, 16, 384), BF),
            pltpu.VMEM((XDIM * GROUP - 1, 16, 384), BF),
            pltpu.VMEM((16, 384), BF),
            pltpu.VMEM((3, 16, 384), BF),
            pltpu.VMEM((16, 384), BF),
            pltpu.VMEM((XDIM, GROUP, 16, 384), BF),
            pltpu.VMEM((SPAN, D), BF),
            pltpu.VMEM((SPAN, D), BF),
            pltpu.VMEM((SPAN, D), BF),
            pltpu.VMEM((SPAN, D), BF),
            pltpu.VMEM((D, D), BF),
            pltpu.SemaphoreType.DMA((5,)),
            pltpu.SemaphoreType.DMA((copies,)),
            pltpu.SemaphoreType.DMA((copies,)),
        ],
        compiler_params=pltpu.CompilerParams(
            collective_id=0, has_side_effects=True, vmem_limit_bytes=40 * 1024 * 1024
        ),
    )(partner_ids, partner_count, *flat, out_weight)
    return tuple(a.reshape(shape) for a in outs[:4]) + (outs[4],)


def solution(mesh):
    tokens = P("dp", "station", None, None)
    return jax.shard_map(
        local,
        mesh=mesh,
        in_specs=(tokens,) * 4 + (P(), P(), P()),
        out_specs=(tokens,) * 4 + (P("dp", None),),
        check_vma=False,
    )
```
